32 devices in a mesh: groups: 2 (over y), dp: 16 (over z, x, core).
Axes of the slice: x: 2, y: 2, z: 4, core: 2. Of those that a mesh axis runs over, the one named last changes fastest.
Arguments:
- queries: bfloat16 [16384, 4096], P(('groups', 'dp')), parts along dimension 0, may hold values from -100 to 100
- resp_kv: bfloat16 [16384, 2, 512], P(('groups', 'dp')), parts along dimension 0, may hold values from -6 to 6
- prompt_kv: bfloat16 [8192, 2, 512], P(('groups', 'dp')), parts along dimension 0, may hold values from -6 to 6
- groups: int32 [64], P(('groups', 'dp')), parts along dimension 0, may hold values from 0 to 15, as said below
- resp_lengths: int32 [64], P(('groups', 'dp')), parts along dimension 0, may hold values from 64 to 256, as said below
- prompt_lengths: int32 [32], P('groups'), parts along dimension 0, may hold values from 64 to 256, as said below
Outputs:
- attended: bfloat16 [16384, 4096], P(('groups', 'dp')), parts along dimension 0
The draws below stay inside these ranges and needn't reach their ends.
There are 2 independent parts, one for each index of `groups`. The reference program is written for one: setup_inputs(seed, part) draws one part's arguments, and reference() takes and returns one part's arrays. A program takes and returns all parts, laid end to end along the dimension named above; each array names one. Nothing has to cross between parts.
Inputs may be any that keep to these rules, and one draw needn't show every extreme that they name: `groups`: entry n is the prompt whose rows response n reads; some prompts are read by many responses. `resp_lengths`: rows at and after the length are padding. `prompt_lengths`: key rows at and after the length are padding.
All inputs are finite; a program needn't handle non-finite values.
Results may differ from the reference program's by a relative error of at most 0.0043.
Values may be sent and summed in bfloat16 or wider, within the bound.
No kernel may reach another device: no remote copies, remote signals or barrier semaphores. Data moves between devices by JAX's collectives and lax.ppermute only.
A program may use at most 128 MiB of HBM per device.

```python
import math
import jax
import jax.numpy as jnp
from jax import lax

HEADS = 32
KV_HEADS = 4
HEAD_DIM = 128
RLEN = 256
PLEN = 256
PROMPTS = 16
NRESP = 32


def draw_queries(key, part):
    per_group = HEADS // KV_HEADS
    shape = (NRESP, RLEN, KV_HEADS, per_group, HEAD_DIM)
    values = jnp.clip(jax.random.normal(jax.random.fold_in(key, 1), shape, jnp.float32), -4.0, 4.0)
    return values.reshape(NRESP * RLEN, HEADS * HEAD_DIM).astype(jnp.bfloat16)


def draw_resp_kv(key, part):
    shape = (NRESP, RLEN, 2, KV_HEADS, HEAD_DIM)
    values = jnp.clip(jax.random.normal(jax.random.fold_in(key, 2), shape, jnp.float32), -4.0, 4.0)
    return values.reshape(NRESP * RLEN, 2, KV_HEADS * HEAD_DIM).astype(jnp.bfloat16)


def draw_groups(key, part):
    hot_prompts = jax.random.randint(jax.random.fold_in(key, 21), (4,), 0, PROMPTS)
    picked = jax.random.randint(jax.random.fold_in(key, 22), (NRESP,), 0, 4)
    choose_hot = jax.random.randint(jax.random.fold_in(key, 23), (NRESP,), 0, 2)
    spread = jax.random.randint(jax.random.fold_in(key, 24), (NRESP,), 0, PROMPTS)
    chosen = jnp.where(choose_hot == 0, hot_prompts[picked], spread)
    return chosen.at[0].set(0).at[1].set(PROMPTS - 1).astype(jnp.int32)


def draw_resp_lengths(key, part):
    lengths = jax.random.randint(jax.random.fold_in(key, 41), (NRESP,), max(3, RLEN // 4), RLEN + 1)
    position = jax.random.randint(jax.random.fold_in(key, 42), (), 0, NRESP)
    return lengths.at[position].set(RLEN).astype(jnp.int32)


def draw_prompt_lengths(key, part):
    lengths = jax.random.randint(jax.random.fold_in(key, 31), (PROMPTS,), max(1, PLEN // 4), PLEN + 1)
    position = jax.random.randint(jax.random.fold_in(key, 32), (), 0, PROMPTS)
    return lengths.at[position].set(PLEN).astype(jnp.int32)


def levels(own_key, dims, pieces, smallest, top_value):
    loudness = 1.0
    for dim, parts in pieces:
        steps = jax.random.uniform(jax.random.fold_in(jax.random.fold_in(own_key, 6), dim), (parts,), jnp.float32, smallest / len(pieces), top_value / len(pieces))
        loudness = loudness * jnp.repeat(jnp.exp(steps), dims[dim] // parts).reshape((-1,) + (1,) * (len(dims) - 1 - dim))
    return loudness


def centred(rng, shape, deviation, reach, shards=(), kind=jnp.bfloat16):
    drawn = jax.random.normal(rng, shape, jnp.float32) * deviation
    if len(shards) > 0:
        drawn = levels(rng, shape, shards, -0.22, 0.18) * drawn
    return jnp.clip(drawn, min=-reach, max=reach).astype(kind)


def setup_inputs(seed: int = 0, part: int = 0) -> dict:
    key_list = jax.random.split(jax.random.key(seed), 7)
    part_splits = jax.random.split(jax.random.fold_in(key_list[6], part), 7)
    queries = draw_queries(jax.random.fold_in(jax.random.fold_in(key_list[6], part), 71), part)
    resp_kv = draw_resp_kv(jax.random.fold_in(jax.random.fold_in(key_list[6], part), 71), part)
    prompt_kv = centred(part_splits[2], (PROMPTS * PLEN, 2, KV_HEADS * HEAD_DIM), 1.0, 6.0, ((0, 16),))
    groups = draw_groups(jax.random.fold_in(jax.random.fold_in(key_list[6], part), 71), part)
    resp_lengths = draw_resp_lengths(jax.random.fold_in(jax.random.fold_in(key_list[6], part), 71), part)
    prompt_lengths = draw_prompt_lengths(jax.random.fold_in(jax.random.fold_in(key_list[6], part), 71), part)
    return {"queries": queries, "resp_kv": resp_kv, "prompt_kv": prompt_kv, "groups": groups, "resp_lengths": resp_lengths, "prompt_lengths": prompt_lengths}


masked_score = -1e+30

def reference(queries, resp_kv, prompt_kv, groups, resp_lengths, prompt_lengths):
    per_group = HEADS // KV_HEADS
    scaling = 1.0 / math.sqrt(HEAD_DIM)
    count = groups.shape[0]

    def one_response(resp_index):
        first_row = (resp_index * RLEN).astype(jnp.int32)
        query_rows = lax.dynamic_slice_in_dim(queries, first_row, RLEN, 0).astype(jnp.float32)
        query_rows = query_rows.reshape(RLEN, KV_HEADS, per_group, HEAD_DIM)
        own_rows = lax.dynamic_slice_in_dim(resp_kv, first_row, RLEN, 0).astype(jnp.float32)
        own_rows = own_rows.reshape(RLEN, 2, KV_HEADS, HEAD_DIM)
        prompt_id = groups[resp_index]
        prompt_first = (prompt_id * PLEN).astype(jnp.int32)
        prompt_rows = lax.dynamic_slice_in_dim(prompt_kv, prompt_first, PLEN, 0).astype(jnp.float32)
        prompt_rows = prompt_rows.reshape(PLEN, 2, KV_HEADS, HEAD_DIM)
        prompt_score = jnp.einsum('thgd,khd->hgtk', query_rows, prompt_rows[:, 0]) * scaling
        own_score = jnp.einsum('thgd,khd->hgtk', query_rows, own_rows[:, 0]) * scaling
        live_len = resp_lengths[resp_index]
        row_index = jnp.arange(RLEN, dtype=jnp.int32)[:, None]
        col_index = jnp.arange(RLEN, dtype=jnp.int32)[None, :]
        own_mask = (col_index <= row_index) & (col_index < live_len)
        prompt_mask = jnp.arange(PLEN, dtype=jnp.int32) < prompt_lengths[prompt_id]
        prompt_score = jnp.where(prompt_mask, prompt_score, masked_score)
        own_score = jnp.where(own_mask, own_score, masked_score)
        highest = jnp.maximum(lax.optimization_barrier(jnp.max(prompt_score, axis=-1)), lax.optimization_barrier(jnp.max(own_score, axis=-1)))[..., None]
        prompt_weight = jnp.exp(prompt_score - highest)
        own_weight = jnp.exp(own_score - highest)
        totals = lax.optimization_barrier(jnp.sum(prompt_weight, axis=-1)) + lax.optimization_barrier(jnp.sum(own_weight, axis=-1))
        prompt_probs = lax.optimization_barrier(prompt_weight.astype(jnp.bfloat16)).astype(jnp.float32)
        own_probs = lax.optimization_barrier(own_weight.astype(jnp.bfloat16)).astype(jnp.float32)
        result = jnp.einsum('hgtk,khd->thgd', prompt_probs, prompt_rows[:, 1])
        result = result + jnp.einsum('hgtk,khd->thgd', own_probs, own_rows[:, 1])
        result = result / jnp.transpose(totals, (2, 0, 1))[..., None]
        valid_rows = jnp.arange(RLEN, dtype=jnp.int32)[:, None, None, None] < live_len
        result = jnp.where(valid_rows, result, jnp.float32(0.0))
        return result.reshape(RLEN, HEADS * HEAD_DIM).astype(jnp.bfloat16)
    blocks = lax.map(one_response, jnp.arange(count, dtype=jnp.int32))
    return blocks.reshape(count * RLEN, HEADS * HEAD_DIM)
```

```python
import functools
import math

import jax
import jax.numpy as jnp
from jax import lax
from jax.experimental import pallas as pl
from jax.experimental.pallas import tpu as pltpu
from jax.sharding import PartitionSpec as P

KV_HEADS = 4
HEAD_DIM = 128
TILE = 16
CHUNKS = 1

masked_score = -1e30
FOLD = math.log2(math.e) / math.sqrt(HEAD_DIM)


def pack_kernel(heads, devices, groups_ref, kv_ref, out_ref):
    slots = groups_ref.shape[0]
    tiles = 0
    for part in range(2):
        rows = kv_ref[:, part, :]
        for head in range(heads):
            block = rows[:, head * HEAD_DIM : (head + 1) * HEAD_DIM]
            out_ref[:, tiles * TILE : (tiles + 1) * TILE, :] = block.reshape(devices, TILE, HEAD_DIM)
            tiles += 1
    extra = out_ref.shape[1] - tiles * TILE
    if extra:
        lane = lax.broadcasted_iota(jnp.int32, (devices, extra, HEAD_DIM), 2)
        wanted = jnp.zeros((devices, extra, HEAD_DIM), jnp.float32)
        for slot in range(slots):
            wanted = jnp.where(lane == slot, groups_ref[slot].astype(jnp.float32), wanted)
        out_ref[:, tiles * TILE :, :] = wanted.astype(jnp.bfloat16)


def select_kernel(slots, rows, in_ref, out_ref, vec_ref, idx_ref, sem):
    devices = in_ref.shape[0]
    wanted = in_ref[:, rows:, :].astype(jnp.float32)
    vec_ref[...] = wanted[:, 0, :].astype(jnp.int32)
    copy = pltpu.make_async_copy(vec_ref, idx_ref, sem)
    copy.start()
    copy.wait()
    for target in range(devices):
        for slot in range(slots):
            out_ref[target, slot] = in_ref[idx_ref[target, slot], :rows, :]


def with_ones(values):
    return jnp.concatenate([values, jnp.ones(values.shape, values.dtype)], axis=1)


def own_kernel(per_group, q_ref, kv_ref, out_ref, lse_ref):
    size = q_ref.shape[0]
    half = size // 2
    keys = kv_ref[:, 0, :]
    values = with_ones(kv_ref[:, 1, :])
    row = lax.broadcasted_iota(jnp.int32, (half, half), 0)
    col = lax.broadcasted_iota(jnp.int32, (half, half), 1)
    causal = col <= row
    lane = lax.broadcasted_iota(jnp.int32, (half, HEAD_DIM), 1)
    for part in range(2):
        rows = slice(part * half, (part + 1) * half)
        seen = (part + 1) * half
        logs = jnp.zeros((half, HEAD_DIM), jnp.float32)
        for head in range(per_group):
            cols = slice(head * HEAD_DIM, (head + 1) * HEAD_DIM)
            score = lax.dot_general(
                q_ref[rows, cols],
                keys[:seen],
                (((1,), (1,)), ((), ())),
                preferred_element_type=jnp.float32,
            )
            last = jnp.where(causal, score[:, seen - half :], masked_score)
            score = last if part == 0 else jnp.concatenate([score[:, :half], last], axis=1)
            highest = jnp.max(score, axis=1, keepdims=True) * FOLD
            weight = jnp.exp2(score * FOLD - highest).astype(jnp.bfloat16)
            sums = jnp.dot(weight, values[:seen], preferred_element_type=jnp.float32)
            totals = sums[:, HEAD_DIM:]
            out_ref[rows, cols] = (sums[:, :HEAD_DIM] / totals).astype(out_ref.dtype)
            logs = jnp.where(lane == head, highest + jnp.log2(totals), logs)
        lse_ref[rows, :] = logs


def prompt_kernel(per_group, first, *refs):
    groups_ref, lives_ref, plens_ref, q_ref, own_ref, lse_ref, k_ref, v_ref = refs[:8]
    out_ref = refs[-1]
    size = q_ref.shape[0]
    half = size // 2
    slot = pl.program_id(0)
    keys = k_ref[...].reshape(-1, HEAD_DIM)
    values = with_ones(v_ref[...].reshape(-1, HEAD_DIM))
    live = plens_ref[groups_ref[slot]]
    rows_live = lives_ref[slot]
    plen = keys.shape[0]
    mask = lax.broadcasted_iota(jnp.int32, (half, plen), 1) < live
    for part in range(2):
        rows = slice(part * half, (part + 1) * half)
        row = lax.broadcasted_iota(jnp.int32, (half, HEAD_DIM), 0) + part * half
        kept = row < rows_live
        for head in range(per_group):
            cols = slice(head * HEAD_DIM, (head + 1) * HEAD_DIM)
            score = lax.dot_general(
                q_ref[rows, cols],
                keys,
                (((1,), (1,)), ((), ())),
                preferred_element_type=jnp.float32,
            )
            score = jnp.where(mask, score, masked_score)
            own_log = lse_ref[rows, head : head + 1]
            highest = jnp.maximum(jnp.max(score, axis=1, keepdims=True) * FOLD, own_log)
            weight = jnp.exp2(score * FOLD - highest).astype(jnp.bfloat16)
            sums = jnp.dot(weight, values, preferred_element_type=jnp.float32)
            scale = jnp.exp2(own_log - highest)
            total = sums[:, HEAD_DIM:] + scale
            result = (sums[:, :HEAD_DIM] + scale * own_ref[rows, cols].astype(jnp.float32)) / total
            out_ref[rows, cols] = jnp.where(kept, result, 0.0).astype(out_ref.dtype)


def params(mib=40):
    return pltpu.CompilerParams(vmem_limit_bytes=mib * 1024 * 1024)


def fetch_fast(prompt_kv, groups, devices):
    slots = groups.shape[0]
    prompt_len = prompt_kv.shape[0]
    heads = KV_HEADS
    rows = 2 * heads * TILE
    extra = 8
    smem = pl.BlockSpec(memory_space=pltpu.SMEM)
    vmem = pl.BlockSpec(memory_space=pltpu.VMEM)
    packed = pl.pallas_call(
        functools.partial(pack_kernel, heads, devices),
        out_shape=jax.ShapeDtypeStruct((devices, rows + extra, HEAD_DIM), jnp.bfloat16),
        in_specs=[smem, vmem],
        out_specs=vmem,
        name="pack",
    )(groups, prompt_kv)
    spread = lax.all_to_all(packed, "dp", split_axis=0, concat_axis=0, tiled=True)
    chosen = pl.pallas_call(
        functools.partial(select_kernel, slots, rows),
        out_shape=jax.ShapeDtypeStruct((devices, slots, rows, HEAD_DIM), jnp.bfloat16),
        in_specs=[vmem],
        out_specs=vmem,
        scratch_shapes=[
            pltpu.VMEM((devices, HEAD_DIM), jnp.int32),
            pltpu.SMEM((devices, HEAD_DIM), jnp.int32),
            pltpu.SemaphoreType.DMA,
        ],
        name="select",
    )(spread)
    return lax.all_to_all(chosen, "dp", split_axis=0, concat_axis=0, tiled=True)


def fetch_plain(prompt_kv, groups, devices):
    slots = groups.shape[0]
    prompt_len, _, width = prompt_kv.shape
    sliver = prompt_len // devices
    wanted = lax.all_gather(groups, "dp", axis=0, tiled=True)
    by_prompt = lax.all_to_all(
        prompt_kv.reshape(devices, sliver, 2, width), "dp", split_axis=0, concat_axis=0, tiled=True
    )
    chosen = jnp.take(by_prompt, wanted, axis=0).reshape(devices, slots, sliver, 2, width)
    fetched = lax.all_to_all(chosen, "dp", split_axis=0, concat_axis=0, tiled=True)
    whole = jnp.transpose(fetched, (1, 0, 2, 3, 4)).reshape(slots, -1, TILE, 2, KV_HEADS, HEAD_DIM)
    whole = jnp.transpose(whole, (1, 0, 3, 4, 2, 5))
    return whole.reshape(whole.shape[0], slots, 2 * KV_HEADS * TILE, HEAD_DIM)


def on_device(queries, resp_kv, prompt_kv, groups, resp_lengths, prompt_lengths):
    devices = lax.axis_size("dp")
    slots = groups.shape[0]
    resp_len = queries.shape[0] // slots
    width = queries.shape[1] // KV_HEADS
    per_group = width // HEAD_DIM
    prompt_len = prompt_kv.shape[0]
    if prompt_len == devices * TILE:
        fetched = fetch_fast(prompt_kv, groups, devices)
    else:
        fetched = fetch_plain(prompt_kv, groups, devices)
    blocks = fetched.shape[0]

    q_spec = pl.BlockSpec((resp_len, width), lambda s, c, *_: (s, c))
    log_spec = pl.BlockSpec((resp_len, HEAD_DIM), lambda s, c, *_: (s, c))
    scores = queries.shape[0] * queries.shape[1] // HEAD_DIM * resp_len
    own, logs = pl.pallas_call(
        functools.partial(own_kernel, per_group),
        grid=(slots, KV_HEADS),
        out_shape=(
            jax.ShapeDtypeStruct(queries.shape, jnp.bfloat16),
            jax.ShapeDtypeStruct((queries.shape[0], KV_HEADS * HEAD_DIM), jnp.float32),
        ),
        in_specs=[q_spec, pl.BlockSpec((resp_len, 2, HEAD_DIM), lambda s, c: (s, 0, c))],
        out_specs=(q_spec, log_spec),
        compiler_params=params(),
        cost_estimate=pl.CostEstimate(
            flops=scores * HEAD_DIM * 4, bytes_accessed=queries.size * 4, transcendentals=scores
        ),
        name="own",
    )(queries, resp_kv)

    def tile_spec(offset):
        return pl.BlockSpec(
            (blocks, None, TILE, HEAD_DIM), lambda s, c, *_: (0, s, c + offset, 0)
        )

    return pl.pallas_call(
        functools.partial(prompt_kernel, per_group, 0),
        grid_spec=pltpu.PrefetchScalarGridSpec(
            num_scalar_prefetch=3,
            grid=(slots, KV_HEADS),
            in_specs=[q_spec, q_spec, log_spec, tile_spec(0), tile_spec(KV_HEADS)],
            out_specs=q_spec,
        ),
        out_shape=jax.ShapeDtypeStruct(queries.shape, jnp.bfloat16),
        compiler_params=params(),
        cost_estimate=pl.CostEstimate(
            flops=scores * HEAD_DIM * 4, bytes_accessed=queries.size * 6, transcendentals=scores
        ),
        name="prompt",
    )(groups, resp_lengths, prompt_lengths, queries, own, logs, fetched, fetched)


def solution(mesh):
    return jax.shard_map(
        on_device,
        mesh=mesh,
        in_specs=(
            P(("groups", "dp"), None),
            P(("groups", "dp"), None, None),
            P(("groups", "dp"), None, None),
            P(("groups", "dp")),
            P(("groups", "dp")),
            P("groups"),
        ),
        out_specs=P(("groups", "dp"), None),
        check_vma=False,
    )
```

```python
import functools
import math

import jax
import jax.numpy as jnp
from jax import lax
from jax.experimental import pallas as pl
from jax.experimental.pallas import tpu as pltpu
from jax.sharding import PartitionSpec as P

KV_HEADS = 4
HEAD_DIM = 128
TILE = 16

masked_score = -1e30
FOLD = math.log2(math.e) / math.sqrt(HEAD_DIM)


def split_pairs(pairs):
    count = pairs.shape[0]
    half = count // 2
    row = lax.broadcasted_iota(jnp.int32, (count, count), 0)
    col = lax.broadcasted_iota(jnp.int32, (count, count), 1)
    source = jnp.where(row < half, 2 * row, 2 * (row - half) + 1)
    chosen = jnp.where(col == source, 1.0, 0.0).astype(pairs.dtype)
    return jnp.dot(chosen, pairs, preferred_element_type=jnp.float32).astype(pairs.dtype)


def pack_kernel(heads, devices, groups_ref, kv_ref, out_ref):
    slots = groups_ref.shape[0]
    count = kv_ref.shape[0]
    head = pl.program_id(0)
    split = split_pairs(kv_ref[...].reshape(2 * count, HEAD_DIM))
    for part in range(2):
        first = pl.multiple_of((part * heads + head) * TILE, TILE)
        out_ref[:, pl.ds(first, TILE), :] = split[part * count : (part + 1) * count].reshape(
            devices, TILE, HEAD_DIM
        )
    rows = 2 * heads * TILE
    extra = out_ref.shape[1] - rows
    if extra:

        @pl.when(head == 0)
        def _():
            lane = lax.broadcasted_iota(jnp.int32, (devices, extra, HEAD_DIM), 2)
            wanted = jnp.zeros((devices, extra, HEAD_DIM), jnp.float32)
            for slot in range(slots):
                wanted = jnp.where(lane == slot, groups_ref[slot].astype(jnp.float32), wanted)
            out_ref[:, rows:, :] = wanted.astype(jnp.bfloat16)


def select_kernel(slots, rows, in_ref, after_ref, out_ref, vec_ref, idx_ref, sem, sems):
    wanted = in_ref[:, rows:, :].astype(jnp.float32)
    vec_ref[...] = wanted[:, 0, :].astype(jnp.int32)
    copy = pltpu.make_async_copy(vec_ref, idx_ref, sem)
    copy.start()
    copy.wait()
    copies = []
    for target in range(in_ref.shape[0]):
        for slot in range(slots):
            copies.append(
                pltpu.make_async_copy(
                    in_ref.at[idx_ref[target, slot], pl.ds(0, rows)],
                    out_ref.at[target, slot],
                    sems.at[target, slot],
                )
            )
            copies[-1].start()
    for copy in copies:
        copy.wait()


def scores_of(keys, queries):
    return lax.dot_general(
        keys, queries, (((1,), (1,)), ((), ())), preferred_element_type=jnp.float32
    )


def with_ones(values):
    turned = jnp.transpose(values)
    return jnp.concatenate([turned, jnp.ones((TILE, turned.shape[1]), turned.dtype)], axis=0)


def own_kernel(per_group, q_ref, kv_ref, *refs):
    out_ref, top_ref, sum_ref = refs[-3:]
    size = q_ref.shape[0]
    half = size // 2
    split = split_pairs(kv_ref[...].reshape(2 * size, HEAD_DIM))
    keys = split[:size]
    values = with_ones(split[size:])
    key = lax.broadcasted_iota(jnp.int32, (half, half), 0)
    row = lax.broadcasted_iota(jnp.int32, (half, half), 1)
    causal = key <= row
    nothing = jnp.zeros((half, half), jnp.bfloat16)
    score, weight = {}, {}
    for step in range(per_group + 2):
        if step < per_group:
            score[step] = scores_of(keys, q_ref[:, step * HEAD_DIM : (step + 1) * HEAD_DIM])
        head = step - 2
        if head >= 0:
            sums = jnp.dot(values, weight.pop(head), preferred_element_type=jnp.float32)
            out_ref[head] = sums[:HEAD_DIM]
            sum_ref[head : head + 1, :] = sums[HEAD_DIM : HEAD_DIM + 1]
        head = step - 1
        if 0 <= head < per_group:
            raw = score.pop(head)
            early = jnp.where(causal, raw[:half, :half], masked_score)
            before = raw[:half, half:]
            late = jnp.where(causal, raw[half:, half:], masked_score)
            top_early = jnp.max(early, axis=0, keepdims=True) * FOLD
            top_late = jnp.max(jnp.maximum(before, late), axis=0, keepdims=True) * FOLD
            top_ref[head : head + 1, :half] = top_early
            top_ref[head : head + 1, half:] = top_late
            early = jnp.exp2(early * FOLD - top_early).astype(jnp.bfloat16)
            before = jnp.exp2(before * FOLD - top_late).astype(jnp.bfloat16)
            late = jnp.exp2(late * FOLD - top_late).astype(jnp.bfloat16)
            weight[head] = jnp.concatenate(
                [
                    jnp.concatenate([early, before], axis=1),
                    jnp.concatenate([nothing, late], axis=1),
                ],
                axis=0,
            )


def prompt_kernel(per_group, *refs):
    groups_ref, lives_ref, plens_ref, q_ref, own_ref, top_ref, sum_ref, k_ref, v_ref = refs[:9]
    out_ref = refs[-1]
    size = q_ref.shape[0]
    slot = pl.program_id(0)
    live = plens_ref[groups_ref[slot]]
    rows_live = lives_ref[slot]
    keys = k_ref[...].reshape(-1, HEAD_DIM)
    dead = lax.broadcasted_iota(jnp.int32, keys.shape, 0) >= live
    keys = jnp.where(dead, keys[:1].astype(jnp.float32), keys.astype(jnp.float32)).astype(keys.dtype)
    values = with_ones(v_ref[...].reshape(-1, HEAD_DIM))
    dead = lax.broadcasted_iota(jnp.int32, values.shape, 1) >= live
    values = jnp.where(dead, 0.0, values.astype(jnp.float32)).astype(values.dtype)
    kept = lax.broadcasted_iota(jnp.int32, (1, size), 1) < rows_live
    score, weight, rows = {}, {}, {}
    for step in range(per_group + 2):
        if step < per_group:
            score[step] = scores_of(keys, q_ref[:, step * HEAD_DIM : (step + 1) * HEAD_DIM])
        head = step - 2
        if head >= 0:
            sums = jnp.dot(values, weight.pop(head), preferred_element_type=jnp.float32)
            scale = rows.pop(head)
            total = sums[HEAD_DIM : HEAD_DIM + 1] + scale * sum_ref[head : head + 1, :]
            share = jnp.where(kept, 1.0 / total, 0.0)
            result = sums[:HEAD_DIM] * share + own_ref[head] * (scale * share)
            out_ref[:, head * HEAD_DIM : (head + 1) * HEAD_DIM] = jnp.transpose(result).astype(
                out_ref.dtype
            )
        head = step - 1
        if 0 <= head < per_group:
            raw = score.pop(head)
            parts = []
            for part in range(2):
                cols = slice(part * HEAD_DIM, (part + 1) * HEAD_DIM)
                piece = raw[:, cols]
                own_top = top_ref[head : head + 1, cols]
                top = jnp.maximum(jnp.max(piece, axis=0, keepdims=True) * FOLD, own_top)
                parts.append(
                    (
                        jnp.exp2(piece * FOLD - top).astype(jnp.bfloat16),
                        jnp.exp2(own_top - top),
                    )
                )
            weight[head] = jnp.concatenate([p[0] for p in parts], axis=1)
            rows[head] = jnp.concatenate([p[1] for p in parts], axis=1)


def params(mib=60):
    return pltpu.CompilerParams(vmem_limit_bytes=mib * 1024 * 1024)


def fetch_fast(prompt_kv, groups, devices, after):
    slots = groups.shape[0]
    prompt_len = prompt_kv.shape[0]
    rows = 2 * KV_HEADS * TILE
    smem = pl.BlockSpec(memory_space=pltpu.SMEM)
    vmem = pl.BlockSpec(memory_space=pltpu.VMEM)
    anywhere = pl.BlockSpec(memory_space=pl.ANY)
    packed = pl.pallas_call(
        functools.partial(pack_kernel, KV_HEADS, devices),
        out_shape=jax.ShapeDtypeStruct((devices, rows + 8, HEAD_DIM), jnp.bfloat16),
        grid=(KV_HEADS,),
        in_specs=[smem, pl.BlockSpec((prompt_len, 2, HEAD_DIM), lambda h: (0, 0, h))],
        out_specs=pl.BlockSpec((devices, rows + 8, HEAD_DIM), lambda h: (0, 0, 0)),
        name="pack",
    )(groups, prompt_kv)
    with jax.named_scope("spread"):
        spread = lax.all_to_all(packed, "dp", split_axis=0, concat_axis=0, tiled=True)
    chosen = pl.pallas_call(
        functools.partial(select_kernel, slots, rows),
        out_shape=jax.ShapeDtypeStruct((devices, slots, rows, HEAD_DIM), jnp.bfloat16),
        in_specs=[vmem, anywhere],
        out_specs=anywhere,
        scratch_shapes=[
            pltpu.VMEM((devices, HEAD_DIM), jnp.int32),
            pltpu.SMEM((devices, HEAD_DIM), jnp.int32),
            pltpu.SemaphoreType.DMA,
            pltpu.SemaphoreType.DMA((devices, slots)),
        ],
        compiler_params=params(4),
        name="select",
    )(spread, pltpu.with_memory_space_constraint(after, pltpu.HBM))
    with jax.named_scope("send"):
        return lax.all_to_all(chosen, "dp", split_axis=0, concat_axis=0, tiled=True)


def fetch_plain(prompt_kv, groups, devices):
    slots = groups.shape[0]
    prompt_len, _, width = prompt_kv.shape
    sliver = prompt_len // devices
    wanted = lax.all_gather(groups, "dp", axis=0, tiled=True)
    by_prompt = lax.all_to_all(
        prompt_kv.reshape(devices, sliver, 2, width), "dp", split_axis=0, concat_axis=0, tiled=True
    )
    chosen = jnp.take(by_prompt, wanted, axis=0).reshape(devices, slots, sliver, 2, width)
    fetched = lax.all_to_all(chosen, "dp", split_axis=0, concat_axis=0, tiled=True)
    whole = jnp.transpose(fetched, (1, 0, 2, 3, 4))
    whole = whole.reshape(slots, -1, TILE, 2, KV_HEADS, HEAD_DIM)
    whole = jnp.transpose(whole, (1, 0, 3, 4, 2, 5))
    return whole.reshape(whole.shape[0], slots, 2 * KV_HEADS * TILE, HEAD_DIM)


def on_device(queries, resp_kv, prompt_kv, groups, resp_lengths, prompt_lengths):
    devices = lax.axis_size("dp")
    slots = groups.shape[0]
    resp_len = queries.shape[0] // slots
    width = queries.shape[1] // KV_HEADS
    per_group = width // HEAD_DIM
    prompt_len = prompt_kv.shape[0]
    heads = KV_HEADS * per_group
    scores = heads * resp_len * resp_len
    moved = queries.size

    own_shapes = (
        jax.ShapeDtypeStruct((slots, heads, HEAD_DIM, resp_len), jnp.float32),
        jax.ShapeDtypeStruct((slots, heads, resp_len), jnp.float32),
        jax.ShapeDtypeStruct((slots, heads, resp_len), jnp.float32),
    )
    own_steps = []
    for slot in range(slots):
        before = own_steps[-1] if own_steps else ()
        own_steps.append(
            pl.pallas_call(
                functools.partial(own_kernel, per_group),
                grid=(KV_HEADS,),
                out_shape=own_shapes,
                in_specs=[
                    pl.BlockSpec((resp_len, width), lambda c, slot=slot: (slot, c)),
                    pl.BlockSpec((resp_len, 2, HEAD_DIM), lambda c, slot=slot: (slot, 0, c)),
                ]
                + [pl.BlockSpec(memory_space=pl.ANY)] * len(before),
                out_specs=(
                    pl.BlockSpec(
                        (None, per_group, HEAD_DIM, resp_len),
                        lambda c, slot=slot: (slot, c, 0, 0),
                    ),
                    pl.BlockSpec((None, per_group, resp_len), lambda c, slot=slot: (slot, c, 0)),
                    pl.BlockSpec((None, per_group, resp_len), lambda c, slot=slot: (slot, c, 0)),
                ),
                input_output_aliases={2 + i: i for i in range(len(before))},
                compiler_params=params(),
                cost_estimate=pl.CostEstimate(
                    flops=scores * HEAD_DIM * 4,
                    bytes_accessed=moved * 6 // slots,
                    transcendentals=scores,
                ),
                name=f"own{slot}",
            )(queries, resp_kv, *before)
        )
    own = [pltpu.with_memory_space_constraint(part, pltpu.HBM) for part in own_steps[-1]]
    queries = pltpu.with_memory_space_constraint(queries, pltpu.HBM)

    if prompt_len == devices * TILE:
        fetched = fetch_fast(prompt_kv, groups, devices, own_steps[0][1])
    else:
        fetched = fetch_plain(prompt_kv, groups, devices)
    blocks = fetched.shape[0]

    q_spec = pl.BlockSpec((resp_len, width), lambda s, c, *_: (s, c))
    own_spec = pl.BlockSpec((None, per_group, HEAD_DIM, resp_len), lambda s, c, *_: (s, c, 0, 0))
    row_spec = pl.BlockSpec((None, per_group, resp_len), lambda s, c, *_: (s, c, 0))

    def tile_spec(offset):
        return pl.BlockSpec(
            (blocks, None, TILE, HEAD_DIM), lambda s, c, *_: (0, s, c + offset, 0)
        )

    return pl.pallas_call(
        functools.partial(prompt_kernel, per_group),
        grid_spec=pltpu.PrefetchScalarGridSpec(
            num_scalar_prefetch=3,
            grid=(slots, KV_HEADS),
            in_specs=[q_spec, own_spec, row_spec, row_spec, tile_spec(0), tile_spec(KV_HEADS)],
            out_specs=q_spec,
        ),
        out_shape=jax.ShapeDtypeStruct(queries.shape, jnp.bfloat16),
        compiler_params=params(32),
        cost_estimate=pl.CostEstimate(
            flops=slots * scores * HEAD_DIM * 4,
            bytes_accessed=moved * 8,
            transcendentals=slots * scores,
        ),
        name="prompt",
    )(groups, resp_lengths, prompt_lengths, queries, *own, fetched, fetched)


def solution(mesh):
    return jax.shard_map(
        on_device,
        mesh=mesh,
        in_specs=(
            P(("groups", "dp"), None),
            P(("groups", "dp"), None, None),
            P(("groups", "dp"), None, None),
            P(("groups", "dp")),
            P(("groups", "dp")),
            P("groups"),
        ),
        out_specs=P(("groups", "dp"), None),
        check_vma=False,
    )
```

```python
import functools
import math

import jax
import jax.numpy as jnp
from jax import lax
from jax.experimental import pallas as pl
from jax.experimental.pallas import tpu as pltpu
from jax.sharding import PartitionSpec as P

KV_HEADS = 4
HEAD_DIM = 128
TILE = 16

masked_score = -1e30
FOLD = math.log2(math.e) / math.sqrt(HEAD_DIM)
MOST_TOTAL = 2.0**60
PIECE = 2
OWN_PIECE = 4


def split_pairs(pairs):
    count = pairs.shape[0]
    half = count // 2
    row = lax.broadcasted_iota(jnp.int32, (count, count), 0)
    col = lax.broadcasted_iota(jnp.int32, (count, count), 1)
    source = jnp.where(row < half, 2 * row, 2 * (row - half) + 1)
    chosen = jnp.where(col == source, 1.0, 0.0).astype(pairs.dtype)
    return jnp.dot(chosen, pairs, preferred_element_type=jnp.float32).astype(pairs.dtype)


def select_kernel(half, place_ref, in_ref, after_ref, first_ref, *refs):
    by_distance, (vec_ref, idx_ref, sem, sems) = refs[:half], refs[half:]
    rows = first_ref.shape[1]
    wanted = in_ref[:, rows:, :].astype(jnp.float32)
    vec_ref[...] = wanted[:, 0, :].astype(jnp.int32)
    copy = pltpu.make_async_copy(vec_ref, idx_ref, sem)
    copy.start()
    copy.wait()
    place = place_ref[0]
    start = place_ref[1]
    copies = []
    for k in range(half):
        for slot, target, out in (
            (0, k, first_ref.at[k]),
            (1, jnp.bitwise_xor(place, k), by_distance[k]),
        ):
            copies.append(
                pltpu.make_async_copy(
                    in_ref.at[idx_ref[start + target, slot], pl.ds(0, rows)], out, sems.at[slot, k]
                )
            )
            copies[-1].start()
    for copy in copies:
        copy.wait()


def scores_of(queries, keys):
    return lax.dot_general(
        queries, keys, (((1,), (1,)), ((), ())), preferred_element_type=jnp.float32
    )


def with_ones(values):
    return jnp.concatenate([values, jnp.ones(values.shape, values.dtype)], axis=1)


def stacked(ref, rows, heads):
    return jnp.concatenate(
        [ref[rows, head * HEAD_DIM : (head + 1) * HEAD_DIM] for head in heads], axis=0
    )


def own_kernel(per_group, q_ref, kv_ref, *refs):
    out_ref, sum_ref = refs[-2:]
    size = q_ref.shape[0]
    half = size // 2
    split = split_pairs(kv_ref[...].reshape(2 * size, HEAD_DIM))
    keys = split[:size]
    values = with_ones(split[size:])
    causal = lax.broadcasted_iota(jnp.int32, (half, half), 1) <= lax.broadcasted_iota(
        jnp.int32, (half, half), 0
    )
    causal = jnp.concatenate([causal.astype(jnp.float32)] * OWN_PIECE, axis=0) > 0.5
    lane = lax.broadcasted_iota(jnp.int32, (half, HEAD_DIM), 1)
    totals = [jnp.ones((half, HEAD_DIM), jnp.float32)] * 2
    pieces = [
        (part, range(first, first + OWN_PIECE))
        for first in range(0, per_group, OWN_PIECE)
        for part in range(2)
    ]
    score, weight = {}, {}
    for step in range(len(pieces) + 2):
        if step < len(pieces):
            part, heads = pieces[step]
            rows = slice(part * half, (part + 1) * half)
            score[step] = scores_of(stacked(q_ref, rows, heads), keys[: (part + 1) * half])
        if step >= 2:
            part, heads = pieces[step - 2]
            sums = jnp.dot(
                weight.pop(step - 2), values[: (part + 1) * half], preferred_element_type=jnp.float32
            )
            for place, head in enumerate(heads):
                rows = slice(place * half, (place + 1) * half)
                out_ref[part * half : (part + 1) * half, head * HEAD_DIM : (head + 1) * HEAD_DIM] = (
                    sums[rows, :HEAD_DIM].astype(out_ref.dtype)
                )
                totals[part] = jnp.where(lane == head, sums[rows, HEAD_DIM:], totals[part])
        if 1 <= step <= len(pieces):
            part, heads = pieces[step - 1]
            raw = score.pop(step - 1)
            last = jnp.where(causal, jnp.exp2(raw[:, part * half :] * FOLD), 0.0).astype(jnp.bfloat16)
            if part:
                before = jnp.exp2(raw[:, :half] * FOLD).astype(jnp.bfloat16)
                last = jnp.concatenate([before, last], axis=1)
            weight[step - 1] = last
    for part in range(2):
        sum_ref[part * half : (part + 1) * half, :] = totals[part]


def prompt_kernel(per_group, slot, count, *refs):
    place_ref, groups_ref, lives_ref, plens_ref, q_ref, kv_ref, own_ref, sum_ref = refs[:8]
    blocks, (out_ref, pairs_ref, sem) = refs[8 : 8 + 2 * count], refs[-3:]
    size = q_ref.shape[0]
    live = plens_ref[groups_ref[slot]]
    rows_live = lives_ref[slot]
    keys, values = (
        jnp.concatenate([ref[...].reshape(-1, HEAD_DIM) for ref in part], axis=0)
        for part in (blocks[:count], blocks[count:])
    )
    position = lax.broadcasted_iota(jnp.int32, (keys.shape[0], HEAD_DIM), 0)
    if count > 1:
        sliver = keys.shape[0] // count
        position = jnp.bitwise_xor(position, place_ref[0] * sliver)
    keys = jnp.where(position < live, keys.astype(jnp.float32), 0.0).astype(keys.dtype)
    alive = jnp.where(position < live, 1.0, 0.0)
    values = jnp.concatenate(
        [values.astype(jnp.float32) * alive, alive], axis=1
    ).astype(values.dtype)
    kept = lax.broadcasted_iota(jnp.int32, (size, HEAD_DIM), 0) < rows_live
    pieces = [range(first, first + PIECE) for first in range(0, per_group, PIECE)]
    score, weight = {}, {}
    most = jnp.zeros((8, HEAD_DIM), jnp.float32)
    least = jnp.min(sum_ref[...].reshape(-1, 8, HEAD_DIM), axis=0)
    for step in range(len(pieces) + 2):
        if step < len(pieces):
            score[step] = scores_of(stacked(q_ref, slice(None), pieces[step]), keys)
        if step >= 2:
            sums = jnp.dot(weight.pop(step - 2), values, preferred_element_type=jnp.float32)
            for place, head in enumerate(pieces[step - 2]):
                rows = slice(place * size, (place + 1) * size)
                cols = slice(head * HEAD_DIM, (head + 1) * HEAD_DIM)
                total = sums[rows, HEAD_DIM:] + sum_ref[:, head : head + 1]
                most = jnp.maximum(most, jnp.max(total.reshape(-1, 8, HEAD_DIM), axis=0))
                result = (sums[rows, :HEAD_DIM] + own_ref[:, cols].astype(jnp.float32)) / total
                out_ref[:, cols] = jnp.where(kept, result, 0.0).astype(out_ref.dtype)
        if 1 <= step <= len(pieces):
            weight[step - 1] = jnp.exp2(score.pop(step - 1) * FOLD).astype(jnp.bfloat16)
    sound = jnp.logical_and(least > 1.0 / MOST_TOTAL, most < MOST_TOTAL)

    @pl.when(jnp.min(jnp.where(sound, 1.0, 0.0)) < 0.5)
    def _():
        first = pl.multiple_of(pl.program_id(0) * HEAD_DIM, HEAD_DIM)
        copy = pltpu.make_async_copy(
            kv_ref.at[pl.ds(slot * size, size), :, pl.ds(first, HEAD_DIM)], pairs_ref, sem
        )
        copy.start()
        copy.wait()
        split = split_pairs(pairs_ref[...].reshape(2 * size, HEAD_DIM))
        own_keys = split[:size]
        own_values = with_ones(split[size:])
        row = lax.broadcasted_iota(jnp.int32, (size, size), 0)
        key = lax.broadcasted_iota(jnp.int32, (size, size), 1)

        def exact(head, carry):
            cols = pl.ds(pl.multiple_of(head * HEAD_DIM, HEAD_DIM), HEAD_DIM)
            queries = q_ref[:, cols]
            prompt = scores_of(queries, keys)
            key_place = lax.broadcasted_iota(jnp.int32, prompt.shape, 1)
            if count > 1:
                key_place = jnp.bitwise_xor(key_place, place_ref[0] * sliver)
            prompt = jnp.where(key_place < live, prompt, masked_score)
            own = jnp.where(key <= row, scores_of(queries, own_keys), masked_score)
            top = FOLD * jnp.maximum(
                jnp.max(prompt, axis=1, keepdims=True), jnp.max(own, axis=1, keepdims=True)
            )
            sums = jnp.dot(
                jnp.exp2(prompt * FOLD - top).astype(jnp.bfloat16),
                values,
                preferred_element_type=jnp.float32,
            )
            sums += jnp.dot(
                jnp.exp2(own * FOLD - top).astype(jnp.bfloat16),
                own_values,
                preferred_element_type=jnp.float32,
            )
            result = sums[:, :HEAD_DIM] / sums[:, HEAD_DIM:]
            out_ref[:, cols] = jnp.where(kept, result, 0.0).astype(out_ref.dtype)
            return carry

        lax.fori_loop(0, per_group, exact, 0)


def params(mib=60):
    return pltpu.CompilerParams(vmem_limit_bytes=mib * 1024 * 1024)


def fetch_fast(prompt_kv, groups, devices, after):
    slots = groups.shape[0]
    prompt_len = prompt_kv.shape[0]
    half = devices // 2
    rows = 2 * KV_HEADS * (prompt_len // half)
    smem = pl.BlockSpec(memory_space=pltpu.SMEM)
    vmem = pl.BlockSpec(memory_space=pltpu.VMEM)
    anywhere = pl.BlockSpec(memory_space=pl.ANY)
    slivers = prompt_kv.reshape(half, prompt_len // half, 2, KV_HEADS, HEAD_DIM)
    slivers = jnp.transpose(slivers, (0, 2, 3, 1, 4)).reshape(half, rows, HEAD_DIM)
    wanted = jnp.pad(groups.astype(jnp.bfloat16), (0, HEAD_DIM - slots))
    wanted = jnp.broadcast_to(wanted, (devices, 8, HEAD_DIM))
    packed = jnp.concatenate([jnp.concatenate([slivers, slivers], axis=0), wanted], axis=1)
    spread = lax.all_to_all(packed, "dp", split_axis=0, concat_axis=0, tiled=True)
    index = lax.axis_index("dp")
    place = lax.rem(index, half)
    piece = jax.ShapeDtypeStruct((rows, HEAD_DIM), jnp.bfloat16)
    first, *rest = pl.pallas_call(
        functools.partial(select_kernel, half),
        out_shape=[jax.ShapeDtypeStruct((half, rows, HEAD_DIM), jnp.bfloat16)] + [piece] * half,
        in_specs=[smem, vmem, anywhere],
        out_specs=[anywhere] * (1 + half),
        scratch_shapes=[
            pltpu.VMEM((devices, HEAD_DIM), jnp.int32),
            pltpu.SMEM((devices, HEAD_DIM), jnp.int32),
            pltpu.SemaphoreType.DMA,
            pltpu.SemaphoreType.DMA((slots, half)),
        ],
        compiler_params=params(4),
        name="select",
    )(
        jnp.stack([place, index - place]),
        spread,
        pltpu.with_memory_space_constraint(after, pltpu.HBM),
    )
    halves = [list(range(half)), list(range(half, devices))]
    first = lax.all_to_all(
        first, "dp", split_axis=0, concat_axis=0, tiled=True, axis_index_groups=halves
    )
    for k in range(1, half):
        rest[k] = lax.ppermute(rest[k], "dp", [(i, i ^ k) for i in range(devices)])
    return [[first], rest], place


def fetch_plain(prompt_kv, groups, devices):
    slots = groups.shape[0]
    prompt_len, _, width = prompt_kv.shape
    sliver = prompt_len // devices
    wanted = lax.all_gather(groups, "dp", axis=0, tiled=True)
    by_prompt = lax.all_to_all(
        prompt_kv.reshape(devices, sliver, 2, width), "dp", split_axis=0, concat_axis=0, tiled=True
    )
    chosen = jnp.take(by_prompt, wanted, axis=0).reshape(devices, slots, sliver, 2, width)
    fetched = lax.all_to_all(chosen, "dp", split_axis=0, concat_axis=0, tiled=True)
    whole = jnp.transpose(fetched, (1, 0, 2, 3, 4))
    whole = whole.reshape(slots, -1, TILE, 2, KV_HEADS, HEAD_DIM)
    whole = jnp.transpose(whole, (1, 0, 3, 4, 2, 5))
    whole = whole.reshape(whole.shape[0], slots, 2 * KV_HEADS * TILE, HEAD_DIM)
    return [[whole[:, slot]] for slot in range(slots)], jnp.int32(0)


def on_device(queries, resp_kv, prompt_kv, groups, resp_lengths, prompt_lengths):
    devices = lax.axis_size("dp")
    slots = groups.shape[0]
    resp_len = queries.shape[0] // slots
    width = queries.shape[1] // KV_HEADS
    per_group = width // HEAD_DIM
    prompt_len = prompt_kv.shape[0]
    heads = KV_HEADS * per_group
    scores = heads * resp_len * resp_len
    moved = queries.size

    own_shapes = (
        jax.ShapeDtypeStruct(queries.shape, jnp.bfloat16),
        jax.ShapeDtypeStruct((queries.shape[0], KV_HEADS * HEAD_DIM), jnp.float32),
    )
    own_steps = []
    for slot in range(slots):
        before = own_steps[-1] if own_steps else ()
        own_steps.append(
            pl.pallas_call(
                functools.partial(own_kernel, per_group),
                grid=(KV_HEADS,),
                out_shape=own_shapes,
                in_specs=[
                    pl.BlockSpec((resp_len, width), lambda c, slot=slot: (slot, c)),
                    pl.BlockSpec((resp_len, 2, HEAD_DIM), lambda c, slot=slot: (slot, 0, c)),
                ]
                + [pl.BlockSpec(memory_space=pl.ANY)] * len(before),
                out_specs=(
                    pl.BlockSpec((resp_len, width), lambda c, slot=slot: (slot, c)),
                    pl.BlockSpec((resp_len, HEAD_DIM), lambda c, slot=slot: (slot, c)),
                ),
                input_output_aliases={2 + i: i for i in range(len(before))},
                compiler_params=params(),
                cost_estimate=pl.CostEstimate(
                    flops=scores * HEAD_DIM * 4,
                    bytes_accessed=moved * 6 // slots,
                    transcendentals=scores,
                ),
                name=f"own{slot}",
            )(queries, resp_kv, *before)
        )
    own = [pltpu.with_memory_space_constraint(part, pltpu.HBM) for part in own_steps[-1]]
    queries = pltpu.with_memory_space_constraint(queries, pltpu.HBM)
    resp_kv = pltpu.with_memory_space_constraint(resp_kv, pltpu.HBM)

    half = devices // 2
    if slots == 2 and devices & (devices - 1) == 0 and prompt_len % (half * TILE) == 0:
        fetched, place = fetch_fast(prompt_kv, groups, devices, own[1])
    else:
        fetched, place = fetch_plain(prompt_kv, groups, devices)
    place = place.reshape(1)

    out = None
    for slot in range(slots):
        blocks = fetched[slot]
        q_spec = pl.BlockSpec((resp_len, width), lambda c, *_, slot=slot: (slot, c))

        def tile_spec(block, offset):
            rows = block.shape[-2] // (2 * KV_HEADS)
            lead = block.shape[:-2]
            return pl.BlockSpec(
                lead + (rows, HEAD_DIM), lambda c, *_: (0,) * len(lead) + (c + offset, 0)
            )

        out = pl.pallas_call(
            functools.partial(prompt_kernel, per_group, slot, len(blocks)),
            grid_spec=pltpu.PrefetchScalarGridSpec(
                num_scalar_prefetch=4,
                grid=(KV_HEADS,),
                in_specs=[
                    q_spec,
                    pl.BlockSpec(memory_space=pl.ANY),
                    q_spec,
                    pl.BlockSpec((resp_len, HEAD_DIM), lambda c, *_, slot=slot: (slot, c)),
                ]
                + [tile_spec(block, 0) for block in blocks]
                + [tile_spec(block, KV_HEADS) for block in blocks]
                + ([] if out is None else [pl.BlockSpec(memory_space=pl.ANY)]),
                out_specs=q_spec,
                scratch_shapes=[
                    pltpu.VMEM((resp_len, 2, HEAD_DIM), jnp.bfloat16),
                    pltpu.SemaphoreType.DMA,
                ],
            ),
            out_shape=jax.ShapeDtypeStruct(queries.shape, jnp.bfloat16),
            input_output_aliases={} if out is None else {8 + 2 * len(blocks): 0},
            compiler_params=params(32),
            cost_estimate=pl.CostEstimate(
                flops=scores * HEAD_DIM * 4,
                bytes_accessed=moved * 8 // slots,
                transcendentals=scores,
            ),
            name=f"prompt{slot}",
        )(
            place,
            groups,
            resp_lengths,
            prompt_lengths,
            queries,
            resp_kv,
            *own,
            *blocks,
            *blocks,
            *([] if out is None else [out]),
        )
    return out


def solution(mesh):
    return jax.shard_map(
        on_device,
        mesh=mesh,
        in_specs=(
            P(("groups", "dp"), None),
            P(("groups", "dp"), None, None),
            P(("groups", "dp"), None, None),
            P(("groups", "dp")),
            P(("groups", "dp")),
            P("groups"),
        ),
        out_specs=P(("groups", "dp"), None),
        check_vma=False,
    )
```

```python
import functools
import math

import jax
import jax.numpy as jnp
from jax import lax
from jax.experimental import pallas as pl
from jax.experimental.pallas import tpu as pltpu
from jax.sharding import PartitionSpec as P


KV_HEADS = 4
HEAD_DIM = 128
TILE = 16

masked_score = -1e30
FOLD = math.log2(math.e) / math.sqrt(HEAD_DIM)
MOST_TOTAL = 2.0**60
PIECE = 2
OWN_PIECE = 4


def split_pairs(pairs):
    count = pairs.shape[0]
    half = count // 2
    row = lax.broadcasted_iota(jnp.int32, (count, count), 0)
    col = lax.broadcasted_iota(jnp.int32, (count, count), 1)
    source = jnp.where(row < half, 2 * row, 2 * (row - half) + 1)
    chosen = jnp.where(col == source, 1.0, 0.0).astype(pairs.dtype)
    return jnp.dot(chosen, pairs, preferred_element_type=jnp.float32).astype(pairs.dtype)


def select_kernel(half, place_ref, in_ref, after_ref, second_ref, *refs):
    by_distance, (vec_ref, idx_ref, sem, sems) = refs[:half], refs[half:]
    rows = second_ref.shape[1]
    wanted = in_ref[:, rows:, :].astype(jnp.float32)
    vec_ref[...] = wanted[:, 0, :].astype(jnp.int32)
    copy = pltpu.make_async_copy(vec_ref, idx_ref, sem)
    copy.start()
    copy.wait()
    place = place_ref[0]
    start = place_ref[1]
    copies = []
    for k in range(half):
        for slot, target, out in (
            (1, k, second_ref.at[k]),
            (0, jnp.bitwise_xor(place, k), by_distance[k]),
        ):
            copies.append(
                pltpu.make_async_copy(
                    in_ref.at[idx_ref[start + target, slot], pl.ds(0, rows)], out, sems.at[slot, k]
                )
            )
            copies[-1].start()
    for copy in copies:
        copy.wait()


def scores_of(queries, keys):
    return lax.dot_general(
        queries, keys, (((1,), (1,)), ((), ())), preferred_element_type=jnp.float32
    )


def with_ones(values):
    return jnp.concatenate([values, jnp.ones(values.shape, values.dtype)], axis=1)


def stacked(ref, rows, heads):
    return jnp.concatenate(
        [ref[rows, head * HEAD_DIM : (head + 1) * HEAD_DIM] for head in heads], axis=0
    )


def own_kernel(per_group, q_ref, kv_ref, *refs):
    out_ref, sum_ref = refs[-2:]
    size = q_ref.shape[0]
    half = size // 2
    split = split_pairs(kv_ref[...].reshape(2 * size, HEAD_DIM))
    keys = split[:size]
    values = with_ones(split[size:])
    causal = lax.broadcasted_iota(jnp.int32, (half, half), 1) <= lax.broadcasted_iota(
        jnp.int32, (half, half), 0
    )
    causal = jnp.concatenate([causal.astype(jnp.float32)] * OWN_PIECE, axis=0) > 0.5
    lane = lax.broadcasted_iota(jnp.int32, (half, HEAD_DIM), 1)
    totals = [jnp.ones((half, HEAD_DIM), jnp.float32)] * 2
    pieces = [
        (part, range(first, first + OWN_PIECE))
        for first in range(0, per_group, OWN_PIECE)
        for part in range(2)
    ]
    score, weight = {}, {}
    for step in range(len(pieces) + 2):
        if step < len(pieces):
            part, heads = pieces[step]
            rows = slice(part * half, (part + 1) * half)
            score[step] = scores_of(stacked(q_ref, rows, heads), keys[: (part + 1) * half])
        if step >= 2:
            part, heads = pieces[step - 2]
            sums = jnp.dot(
                weight.pop(step - 2), values[: (part + 1) * half], preferred_element_type=jnp.float32
            )
            for place, head in enumerate(heads):
                rows = slice(place * half, (place + 1) * half)
                out_ref[part * half : (part + 1) * half, head * HEAD_DIM : (head + 1) * HEAD_DIM] = (
                    sums[rows, :HEAD_DIM].astype(out_ref.dtype)
                )
                totals[part] = jnp.where(lane == head, sums[rows, HEAD_DIM:], totals[part])
        if 1 <= step <= len(pieces):
            part, heads = pieces[step - 1]
            raw = score.pop(step - 1)
            last = jnp.where(causal, jnp.exp2(raw[:, part * half :] * FOLD), 0.0).astype(jnp.bfloat16)
            if part:
                before = jnp.exp2(raw[:, :half] * FOLD).astype(jnp.bfloat16)
                last = jnp.concatenate([before, last], axis=1)
            weight[step - 1] = last
    for part in range(2):
        sum_ref[part * half : (part + 1) * half, :] = totals[part]


def prompt_kernel(per_group, slot, count, *refs):
    place_ref, groups_ref, lives_ref, plens_ref, q_ref, kv_ref, own_ref, sum_ref = refs[:8]
    blocks, (out_ref, pairs_ref, sem) = refs[8 : 8 + 2 * count], refs[-3:]
    size = q_ref.shape[0]
    live = plens_ref[groups_ref[slot]]
    rows_live = lives_ref[slot]
    keys, values = (
        jnp.concatenate([ref[...].reshape(-1, HEAD_DIM) for ref in part], axis=0)
        for part in (blocks[:count], blocks[count:])
    )
    position = lax.broadcasted_iota(jnp.int32, (keys.shape[0], HEAD_DIM), 0)
    if count > 1:
        sliver = keys.shape[0] // count
        position = jnp.bitwise_xor(position, place_ref[0] * sliver)
    keys = jnp.where(position < live, keys.astype(jnp.float32), 0.0).astype(keys.dtype)
    alive = jnp.where(position < live, 1.0, 0.0)
    values = jnp.concatenate(
        [values.astype(jnp.float32) * alive, alive], axis=1
    ).astype(values.dtype)
    kept = lax.broadcasted_iota(jnp.int32, (size, HEAD_DIM), 0) < rows_live
    pieces = [range(first, first + PIECE) for first in range(0, per_group, PIECE)]
    score, weight = {}, {}
    most = jnp.zeros((8, HEAD_DIM), jnp.float32)
    least = jnp.min(sum_ref[...].reshape(-1, 8, HEAD_DIM), axis=0)
    for step in range(len(pieces) + 2):
        if step < len(pieces):
            score[step] = scores_of(stacked(q_ref, slice(None), pieces[step]), keys)
        if step >= 2:
            sums = jnp.dot(weight.pop(step - 2), values, preferred_element_type=jnp.float32)
            for place, head in enumerate(pieces[step - 2]):
                rows = slice(place * size, (place + 1) * size)
                cols = slice(head * HEAD_DIM, (head + 1) * HEAD_DIM)
                total = sums[rows, HEAD_DIM:] + sum_ref[:, head : head + 1]
                most = jnp.maximum(most, jnp.max(total.reshape(-1, 8, HEAD_DIM), axis=0))
                result = (sums[rows, :HEAD_DIM] + own_ref[:, cols].astype(jnp.float32)) / total
                out_ref[:, cols] = jnp.where(kept, result, 0.0).astype(out_ref.dtype)
        if 1 <= step <= len(pieces):
            weight[step - 1] = jnp.exp2(score.pop(step - 1) * FOLD).astype(jnp.bfloat16)
    sound = jnp.logical_and(least > 1.0 / MOST_TOTAL, most < MOST_TOTAL)

    @pl.when(jnp.min(jnp.where(sound, 1.0, 0.0)) < 0.5)
    def _():
        first = pl.multiple_of(pl.program_id(0) * HEAD_DIM, HEAD_DIM)
        copy = pltpu.make_async_copy(
            kv_ref.at[pl.ds(slot * size, size), :, pl.ds(first, HEAD_DIM)], pairs_ref, sem
        )
        copy.start()
        copy.wait()
        split = split_pairs(pairs_ref[...].reshape(2 * size, HEAD_DIM))
        own_keys = split[:size]
        own_values = with_ones(split[size:])
        row = lax.broadcasted_iota(jnp.int32, (size, size), 0)
        key = lax.broadcasted_iota(jnp.int32, (size, size), 1)

        def exact(head, carry):
            cols = pl.ds(pl.multiple_of(head * HEAD_DIM, HEAD_DIM), HEAD_DIM)
            queries = q_ref[:, cols]
            prompt = scores_of(queries, keys)
            key_place = lax.broadcasted_iota(jnp.int32, prompt.shape, 1)
            if count > 1:
                key_place = jnp.bitwise_xor(key_place, place_ref[0] * sliver)
            prompt = jnp.where(key_place < live, prompt, masked_score)
            own = jnp.where(key <= row, scores_of(queries, own_keys), masked_score)
            top = FOLD * jnp.maximum(
                jnp.max(prompt, axis=1, keepdims=True), jnp.max(own, axis=1, keepdims=True)
            )
            sums = jnp.dot(
                jnp.exp2(prompt * FOLD - top).astype(jnp.bfloat16),
                values,
                preferred_element_type=jnp.float32,
            )
            sums += jnp.dot(
                jnp.exp2(own * FOLD - top).astype(jnp.bfloat16),
                own_values,
                preferred_element_type=jnp.float32,
            )
            result = sums[:, :HEAD_DIM] / sums[:, HEAD_DIM:]
            out_ref[:, cols] = jnp.where(kept, result, 0.0).astype(out_ref.dtype)
            return carry

        lax.fori_loop(0, per_group, exact, 0)


def params(mib=60):
    return pltpu.CompilerParams(vmem_limit_bytes=mib * 1024 * 1024)


def fetch_fast(prompt_kv, groups, devices, after):
    slots = groups.shape[0]
    prompt_len = prompt_kv.shape[0]
    half = devices // 2
    rows = 2 * KV_HEADS * (prompt_len // half)
    smem = pl.BlockSpec(memory_space=pltpu.SMEM)
    vmem = pl.BlockSpec(memory_space=pltpu.VMEM)
    anywhere = pl.BlockSpec(memory_space=pl.ANY)
    slivers = prompt_kv.reshape(half, prompt_len // half, 2, KV_HEADS, HEAD_DIM)
    slivers = jnp.transpose(slivers, (0, 2, 3, 1, 4)).reshape(half, rows, HEAD_DIM)
    wanted = jnp.pad(groups.astype(jnp.bfloat16), (0, HEAD_DIM - slots))
    wanted = jnp.broadcast_to(wanted, (devices, 8, HEAD_DIM))
    packed = jnp.concatenate([jnp.concatenate([slivers, slivers], axis=0), wanted], axis=1)
    spread = lax.all_to_all(packed, "dp", split_axis=0, concat_axis=0, tiled=True)
    index = lax.axis_index("dp")
    place = lax.rem(index, half)
    piece = jax.ShapeDtypeStruct((rows, HEAD_DIM), jnp.bfloat16)
    second, *rest = pl.pallas_call(
        functools.partial(select_kernel, half),
        out_shape=[jax.ShapeDtypeStruct((half, rows, HEAD_DIM), jnp.bfloat16)] + [piece] * half,
        in_specs=[smem, vmem, anywhere],
        out_specs=[anywhere] * (1 + half),
        scratch_shapes=[
            pltpu.VMEM((devices, HEAD_DIM), jnp.int32),
            pltpu.SMEM((devices, HEAD_DIM), jnp.int32),
            pltpu.SemaphoreType.DMA,
            pltpu.SemaphoreType.DMA((slots, half)),
        ],
        compiler_params=params(4),
        name="select",
    )(
        jnp.stack([place, index - place]),
        spread,
        pltpu.with_memory_space_constraint(after, pltpu.HBM),
    )
    halves = [list(range(half)), list(range(half, devices))]
    for k in range(1, half):
        rest[k] = lax.ppermute(rest[k], "dp", [(i, i ^ k) for i in range(devices)])
    second = lax.all_to_all(
        second, "dp", split_axis=0, concat_axis=0, tiled=True, axis_index_groups=halves
    )
    return [rest, [second]], place


def fetch_plain(prompt_kv, groups, devices):
    slots = groups.shape[0]
    prompt_len, _, width = prompt_kv.shape
    sliver = prompt_len // devices
    wanted = lax.all_gather(groups, "dp", axis=0, tiled=True)
    by_prompt = lax.all_to_all(
        prompt_kv.reshape(devices, sliver, 2, width), "dp", split_axis=0, concat_axis=0, tiled=True
    )
    chosen = jnp.take(by_prompt, wanted, axis=0).reshape(devices, slots, sliver, 2, width)
    fetched = lax.all_to_all(chosen, "dp", split_axis=0, concat_axis=0, tiled=True)
    whole = jnp.transpose(fetched, (1, 0, 2, 3, 4))
    whole = whole.reshape(slots, -1, TILE, 2, KV_HEADS, HEAD_DIM)
    whole = jnp.transpose(whole, (1, 0, 3, 4, 2, 5))
    whole = whole.reshape(whole.shape[0], slots, 2 * KV_HEADS * TILE, HEAD_DIM)
    return [[whole[:, slot]] for slot in range(slots)], jnp.int32(0)


def on_device(queries, resp_kv, prompt_kv, groups, resp_lengths, prompt_lengths):
    devices = lax.axis_size("dp")
    slots = groups.shape[0]
    resp_len = queries.shape[0] // slots
    width = queries.shape[1] // KV_HEADS
    per_group = width // HEAD_DIM
    prompt_len = prompt_kv.shape[0]
    heads = KV_HEADS * per_group
    scores = heads * resp_len * resp_len
    moved = queries.size

    own_shapes = (
        jax.ShapeDtypeStruct(queries.shape, jnp.bfloat16),
        jax.ShapeDtypeStruct((queries.shape[0], KV_HEADS * HEAD_DIM), jnp.float32),
    )
    own_steps = []
    for slot in range(slots):
        before = own_steps[-1] if own_steps else ()
        own_steps.append(
            pl.pallas_call(
                functools.partial(own_kernel, per_group),
                grid=(KV_HEADS,),
                out_shape=own_shapes,
                in_specs=[
                    pl.BlockSpec((resp_len, width), lambda c, slot=slot: (slot, c)),
                    pl.BlockSpec((resp_len, 2, HEAD_DIM), lambda c, slot=slot: (slot, 0, c)),
                ]
                + [pl.BlockSpec(memory_space=pl.ANY)] * len(before),
                out_specs=(
                    pl.BlockSpec((resp_len, width), lambda c, slot=slot: (slot, c)),
                    pl.BlockSpec((resp_len, HEAD_DIM), lambda c, slot=slot: (slot, c)),
                ),
                input_output_aliases={2 + i: i for i in range(len(before))},
                compiler_params=params(),
                cost_estimate=pl.CostEstimate(
                    flops=scores * HEAD_DIM * 4,
                    bytes_accessed=moved * 6 // slots,
                    transcendentals=scores,
                ),
            )(queries, resp_kv, *before)
        )
    own = [pltpu.with_memory_space_constraint(part, pltpu.HBM) for part in own_steps[-1]]
    queries = pltpu.with_memory_space_constraint(queries, pltpu.HBM)
    resp_kv = pltpu.with_memory_space_constraint(resp_kv, pltpu.HBM)

    half = devices // 2
    if slots == 2 and devices & (devices - 1) == 0 and prompt_len % (half * TILE) == 0:
        fetched, place = fetch_fast(prompt_kv, groups, devices, own[1])
    else:
        fetched, place = fetch_plain(prompt_kv, groups, devices)
    place = place.reshape(1)

    out = None
    for slot in range(slots):
        blocks = fetched[slot]
        q_spec = pl.BlockSpec((resp_len, width), lambda c, *_, slot=slot: (slot, c))

        def tile_spec(block, offset):
            rows = block.shape[-2] // (2 * KV_HEADS)
            lead = block.shape[:-2]
            return pl.BlockSpec(
                lead + (rows, HEAD_DIM), lambda c, *_: (0,) * len(lead) + (c + offset, 0)
            )

        out = pl.pallas_call(
            functools.partial(prompt_kernel, per_group, slot, len(blocks)),
            grid_spec=pltpu.PrefetchScalarGridSpec(
                num_scalar_prefetch=4,
                grid=(KV_HEADS,),
                in_specs=[
                    q_spec,
                    pl.BlockSpec(memory_space=pl.ANY),
                    q_spec,
                    pl.BlockSpec((resp_len, HEAD_DIM), lambda c, *_, slot=slot: (slot, c)),
                ]
                + [tile_spec(block, 0) for block in blocks]
                + [tile_spec(block, KV_HEADS) for block in blocks]
                + ([] if out is None else [pl.BlockSpec(memory_space=pl.ANY)]),
                out_specs=q_spec,
                scratch_shapes=[
                    pltpu.VMEM((resp_len, 2, HEAD_DIM), jnp.bfloat16),
                    pltpu.SemaphoreType.DMA,
                ],
            ),
            out_shape=jax.ShapeDtypeStruct(queries.shape, jnp.bfloat16),
            input_output_aliases={} if out is None else {8 + 2 * len(blocks): 0},
            compiler_params=params(32),
            cost_estimate=pl.CostEstimate(
                flops=scores * HEAD_DIM * 4,
                bytes_accessed=moved * 8 // slots,
                transcendentals=scores,
            ),
        )(
            place,
            groups,
            resp_lengths,
            prompt_lengths,
            queries,
            resp_kv,
            *own,
            *blocks,
            *blocks,
            *([] if out is None else [out]),
        )
    return out


def solution(mesh):
    return jax.shard_map(
        on_device,
        mesh=mesh,
        in_specs=(
            P(("groups", "dp"), None),
            P(("groups", "dp"), None, None),
            P(("groups", "dp"), None, None),
            P(("groups", "dp")),
            P(("groups", "dp")),
            P("groups"),
        ),
        out_specs=P(("groups", "dp"), None),
        check_vma=False,
    )
```

```python
import functools
import math

import jax
import jax.numpy as jnp
from jax import lax
from jax.experimental import pallas as pl
from jax.experimental.pallas import tpu as pltpu
from jax.sharding import PartitionSpec as P


KV_HEADS = 4
HEAD_DIM = 128
TILE = 16

masked_score = -1e30
FOLD = math.log2(math.e) / math.sqrt(HEAD_DIM)
MOST_TOTAL = 2.0**60
PIECE = 2
OWN_PIECE = 4


def split_pairs(pairs):
    count = pairs.shape[0]
    half = count // 2
    row = lax.broadcasted_iota(jnp.int32, (count, count), 0)
    col = lax.broadcasted_iota(jnp.int32, (count, count), 1)
    source = jnp.where(row < half, 2 * row, 2 * (row - half) + 1)
    chosen = jnp.where(col == source, 1.0, 0.0).astype(pairs.dtype)
    return jnp.dot(chosen, pairs, preferred_element_type=jnp.float32).astype(pairs.dtype)


def select_kernel(half, place_ref, *refs):
    asked, (in_ref, after_ref, second_ref) = refs[:half], refs[half : half + 3]
    by_distance, sems = refs[half + 3 : -1], refs[-1]
    copies = []
    for k in range(half):
        for slot, out in (
            (1, second_ref.at[jnp.bitwise_xor(place_ref[0], k)]),
            (0, by_distance[k]),
        ):
            copies.append(
                pltpu.make_async_copy(in_ref.at[asked[k][slot]], out, sems.at[slot, k])
            )
            copies[-1].start()
    for copy in copies:
        copy.wait()


def scores_of(queries, keys):
    return lax.dot_general(
        queries, keys, (((1,), (1,)), ((), ())), preferred_element_type=jnp.float32
    )


def with_ones(values):
    return jnp.concatenate([values, jnp.ones(values.shape, values.dtype)], axis=1)


def stacked(ref, rows, heads):
    return jnp.concatenate(
        [ref[rows, head * HEAD_DIM : (head + 1) * HEAD_DIM] for head in heads], axis=0
    )


def own_kernel(per_group, q_ref, kv_ref, *refs):
    out_ref, sum_ref = refs[-2:]
    size = q_ref.shape[0]
    half = size // 2
    split = split_pairs(kv_ref[...].reshape(2 * size, HEAD_DIM))
    keys = split[:size]
    values = with_ones(split[size:])
    causal = lax.broadcasted_iota(jnp.int32, (half, half), 1) <= lax.broadcasted_iota(
        jnp.int32, (half, half), 0
    )
    causal = jnp.concatenate([causal.astype(jnp.float32)] * OWN_PIECE, axis=0) > 0.5
    lane = lax.broadcasted_iota(jnp.int32, (half, HEAD_DIM), 1)
    totals = [jnp.ones((half, HEAD_DIM), jnp.float32)] * 2
    pieces = [
        (part, range(first, first + OWN_PIECE))
        for first in range(0, per_group, OWN_PIECE)
        for part in range(2)
    ]
    score, weight = {}, {}
    for step in range(len(pieces) + 2):
        if step < len(pieces):
            part, heads = pieces[step]
            rows = slice(part * half, (part + 1) * half)
            score[step] = scores_of(stacked(q_ref, rows, heads), keys[: (part + 1) * half])
        if step >= 2:
            part, heads = pieces[step - 2]
            sums = jnp.dot(
                weight.pop(step - 2), values[: (part + 1) * half], preferred_element_type=jnp.float32
            )
            for place, head in enumerate(heads):
                rows = slice(place * half, (place + 1) * half)
                out_ref[part * half : (part + 1) * half, head * HEAD_DIM : (head + 1) * HEAD_DIM] = (
                    sums[rows, :HEAD_DIM].astype(out_ref.dtype)
                )
                totals[part] = jnp.where(lane == head, sums[rows, HEAD_DIM:], totals[part])
        if 1 <= step <= len(pieces):
            part, heads = pieces[step - 1]
            raw = score.pop(step - 1)
            last = jnp.where(causal, jnp.exp2(raw[:, part * half :] * FOLD), 0.0).astype(jnp.bfloat16)
            if part:
                before = jnp.exp2(raw[:, :half] * FOLD).astype(jnp.bfloat16)
                last = jnp.concatenate([before, last], axis=1)
            weight[step - 1] = last
    for part in range(2):
        sum_ref[part * half : (part + 1) * half, :] = totals[part]


def prompt_kernel(per_group, slot, count, *refs):
    place_ref, groups_ref, lives_ref, plens_ref, q_ref, kv_ref, own_ref, sum_ref = refs[:8]
    blocks, (out_ref, pairs_ref, sem) = refs[8 : 8 + 2 * count], refs[-3:]
    size = q_ref.shape[0]
    live = plens_ref[groups_ref[slot]]
    rows_live = lives_ref[slot]
    keys, values = (
        jnp.concatenate([ref[...].reshape(-1, HEAD_DIM) for ref in part], axis=0)
        for part in (blocks[:count], blocks[count:])
    )
    position = lax.broadcasted_iota(jnp.int32, (keys.shape[0], HEAD_DIM), 0)
    if count > 1:
        sliver = keys.shape[0] // count
        position = jnp.bitwise_xor(position, place_ref[0] * sliver)
    keys = jnp.where(position < live, keys.astype(jnp.float32), 0.0).astype(keys.dtype)
    alive = jnp.where(position < live, 1.0, 0.0)
    values = jnp.concatenate(
        [values.astype(jnp.float32) * alive, alive], axis=1
    ).astype(values.dtype)
    kept = lax.broadcasted_iota(jnp.int32, (size, HEAD_DIM), 0) < rows_live
    pieces = [range(first, first + PIECE) for first in range(0, per_group, PIECE)]
    score, weight = {}, {}
    most = jnp.zeros((8, HEAD_DIM), jnp.float32)
    least = jnp.min(sum_ref[...].reshape(-1, 8, HEAD_DIM), axis=0)
    for step in range(len(pieces) + 2):
        if step < len(pieces):
            score[step] = scores_of(stacked(q_ref, slice(None), pieces[step]), keys)
        if step >= 2:
            sums = jnp.dot(weight.pop(step - 2), values, preferred_element_type=jnp.float32)
            for place, head in enumerate(pieces[step - 2]):
                rows = slice(place * size, (place + 1) * size)
                cols = slice(head * HEAD_DIM, (head + 1) * HEAD_DIM)
                total = sums[rows, HEAD_DIM:] + sum_ref[:, head : head + 1]
                most = jnp.maximum(most, jnp.max(total.reshape(-1, 8, HEAD_DIM), axis=0))
                result = (sums[rows, :HEAD_DIM] + own_ref[:, cols].astype(jnp.float32)) / total
                out_ref[:, cols] = jnp.where(kept, result, 0.0).astype(out_ref.dtype)
        if 1 <= step <= len(pieces):
            weight[step - 1] = jnp.exp2(score.pop(step - 1) * FOLD).astype(jnp.bfloat16)
    sound = jnp.logical_and(least > 1.0 / MOST_TOTAL, most < MOST_TOTAL)

    @pl.when(jnp.min(jnp.where(sound, 1.0, 0.0)) < 0.5)
    def _():
        first = pl.multiple_of(pl.program_id(0) * HEAD_DIM, HEAD_DIM)
        copy = pltpu.make_async_copy(
            kv_ref.at[pl.ds(slot * size, size), :, pl.ds(first, HEAD_DIM)], pairs_ref, sem
        )
        copy.start()
        copy.wait()
        split = split_pairs(pairs_ref[...].reshape(2 * size, HEAD_DIM))
        own_keys = split[:size]
        own_values = with_ones(split[size:])
        row = lax.broadcasted_iota(jnp.int32, (size, size), 0)
        key = lax.broadcasted_iota(jnp.int32, (size, size), 1)

        def exact(head, carry):
            cols = pl.ds(pl.multiple_of(head * HEAD_DIM, HEAD_DIM), HEAD_DIM)
            queries = q_ref[:, cols]
            prompt = scores_of(queries, keys)
            key_place = lax.broadcasted_iota(jnp.int32, prompt.shape, 1)
            if count > 1:
                key_place = jnp.bitwise_xor(key_place, place_ref[0] * sliver)
            prompt = jnp.where(key_place < live, prompt, masked_score)
            own = jnp.where(key <= row, scores_of(queries, own_keys), masked_score)
            top = FOLD * jnp.maximum(
                jnp.max(prompt, axis=1, keepdims=True), jnp.max(own, axis=1, keepdims=True)
            )
            sums = jnp.dot(
                jnp.exp2(prompt * FOLD - top).astype(jnp.bfloat16),
                values,
                preferred_element_type=jnp.float32,
            )
            sums += jnp.dot(
                jnp.exp2(own * FOLD - top).astype(jnp.bfloat16),
                own_values,
                preferred_element_type=jnp.float32,
            )
            result = sums[:, :HEAD_DIM] / sums[:, HEAD_DIM:]
            out_ref[:, cols] = jnp.where(kept, result, 0.0).astype(out_ref.dtype)
            return carry

        lax.fori_loop(0, per_group, exact, 0)


def params(mib=60):
    return pltpu.CompilerParams(vmem_limit_bytes=mib * 1024 * 1024)


def fetch_fast(prompt_kv, groups, devices, after):
    slots = groups.shape[0]
    prompt_len = prompt_kv.shape[0]
    half = devices // 2
    rows = 2 * KV_HEADS * (prompt_len // half)
    smem = pl.BlockSpec(memory_space=pltpu.SMEM)
    vmem = pl.BlockSpec(memory_space=pltpu.VMEM)
    anywhere = pl.BlockSpec(memory_space=pl.ANY)
    slivers = prompt_kv.reshape(half, prompt_len // half, 2, KV_HEADS, HEAD_DIM)
    slivers = jnp.transpose(slivers, (0, 2, 3, 1, 4)).reshape(half, rows, HEAD_DIM)
    packed = jnp.concatenate([slivers, slivers], axis=0)
    spread = lax.all_to_all(packed, "dp", split_axis=0, concat_axis=0, tiled=True)
    asked = [groups]
    for k in range(1, half):
        asked.append(lax.ppermute(groups, "dp", [(i, i ^ k) for i in range(devices)]))
    index = lax.axis_index("dp")
    place = lax.rem(index, half)
    piece = jax.ShapeDtypeStruct((rows, HEAD_DIM), jnp.bfloat16)
    second, *rest = pl.pallas_call(
        functools.partial(select_kernel, half),
        out_shape=[jax.ShapeDtypeStruct((half, rows, HEAD_DIM), jnp.bfloat16)] + [piece] * half,
        in_specs=[smem] * (1 + half) + [vmem, anywhere],
        out_specs=[anywhere] * (1 + half),
        scratch_shapes=[pltpu.SemaphoreType.DMA((slots, half))],
        compiler_params=params(4),
        name="select",
    )(
        place.reshape(1),
        *asked,
        spread,
        pltpu.with_memory_space_constraint(after, pltpu.HBM),
    )
    halves = [list(range(half)), list(range(half, devices))]
    for k in range(1, half):
        rest[k] = lax.ppermute(rest[k], "dp", [(i, i ^ k) for i in range(devices)])
    second = lax.all_to_all(
        second, "dp", split_axis=0, concat_axis=0, tiled=True, axis_index_groups=halves
    )
    return [rest, [second]], place


def fetch_plain(prompt_kv, groups, devices):
    slots = groups.shape[0]
    prompt_len, _, width = prompt_kv.shape
    sliver = prompt_len // devices
    wanted = lax.all_gather(groups, "dp", axis=0, tiled=True)
    by_prompt = lax.all_to_all(
        prompt_kv.reshape(devices, sliver, 2, width), "dp", split_axis=0, concat_axis=0, tiled=True
    )
    chosen = jnp.take(by_prompt, wanted, axis=0).reshape(devices, slots, sliver, 2, width)
    fetched = lax.all_to_all(chosen, "dp", split_axis=0, concat_axis=0, tiled=True)
    whole = jnp.transpose(fetched, (1, 0, 2, 3, 4))
    whole = whole.reshape(slots, -1, TILE, 2, KV_HEADS, HEAD_DIM)
    whole = jnp.transpose(whole, (1, 0, 3, 4, 2, 5))
    whole = whole.reshape(whole.shape[0], slots, 2 * KV_HEADS * TILE, HEAD_DIM)
    return [[whole[:, slot]] for slot in range(slots)], jnp.int32(0)


def on_device(queries, resp_kv, prompt_kv, groups, resp_lengths, prompt_lengths):
    devices = lax.axis_size("dp")
    slots = groups.shape[0]
    resp_len = queries.shape[0] // slots
    width = queries.shape[1] // KV_HEADS
    per_group = width // HEAD_DIM
    prompt_len = prompt_kv.shape[0]
    heads = KV_HEADS * per_group
    scores = heads * resp_len * resp_len
    moved = queries.size

    own_shapes = (
        jax.ShapeDtypeStruct(queries.shape, jnp.bfloat16),
        jax.ShapeDtypeStruct((queries.shape[0], KV_HEADS * HEAD_DIM), jnp.float32),
    )
    own_steps = []
    for slot in range(slots):
        before = own_steps[-1] if own_steps else ()
        own_steps.append(
            pl.pallas_call(
                functools.partial(own_kernel, per_group),
                grid=(KV_HEADS,),
                out_shape=own_shapes,
                in_specs=[
                    pl.BlockSpec((resp_len, width), lambda c, slot=slot: (slot, c)),
                    pl.BlockSpec((resp_len, 2, HEAD_DIM), lambda c, slot=slot: (slot, 0, c)),
                ]
                + [pl.BlockSpec(memory_space=pl.ANY)] * len(before),
                out_specs=(
                    pl.BlockSpec((resp_len, width), lambda c, slot=slot: (slot, c)),
                    pl.BlockSpec((resp_len, HEAD_DIM), lambda c, slot=slot: (slot, c)),
                ),
                input_output_aliases={2 + i: i for i in range(len(before))},
                compiler_params=params(),
                cost_estimate=pl.CostEstimate(
                    flops=scores * HEAD_DIM * 4,
                    bytes_accessed=moved * 6 // slots,
                    transcendentals=scores,
                ),
            )(queries, resp_kv, *before)
        )
    own = [pltpu.with_memory_space_constraint(part, pltpu.HBM) for part in own_steps[-1]]
    queries = pltpu.with_memory_space_constraint(queries, pltpu.HBM)
    resp_kv = pltpu.with_memory_space_constraint(resp_kv, pltpu.HBM)

    half = devices // 2
    if slots == 2 and devices & (devices - 1) == 0 and prompt_len % (half * TILE) == 0:
        fetched, place = fetch_fast(prompt_kv, groups, devices, own[1])
    else:
        fetched, place = fetch_plain(prompt_kv, groups, devices)
    place = place.reshape(1)

    out = None
    for slot in range(slots):
        blocks = fetched[slot]
        q_spec = pl.BlockSpec((resp_len, width), lambda c, *_, slot=slot: (slot, c))

        def tile_spec(block, offset):
            rows = block.shape[-2] // (2 * KV_HEADS)
            lead = block.shape[:-2]
            return pl.BlockSpec(
                lead + (rows, HEAD_DIM), lambda c, *_: (0,) * len(lead) + (c + offset, 0)
            )

        out = pl.pallas_call(
            functools.partial(prompt_kernel, per_group, slot, len(blocks)),
            grid_spec=pltpu.PrefetchScalarGridSpec(
                num_scalar_prefetch=4,
                grid=(KV_HEADS,),
                in_specs=[
                    q_spec,
                    pl.BlockSpec(memory_space=pl.ANY),
                    q_spec,
                    pl.BlockSpec((resp_len, HEAD_DIM), lambda c, *_, slot=slot: (slot, c)),
                ]
                + [tile_spec(block, 0) for block in blocks]
                + [tile_spec(block, KV_HEADS) for block in blocks]
                + ([] if out is None else [pl.BlockSpec(memory_space=pl.ANY)]),
                out_specs=q_spec,
                scratch_shapes=[
                    pltpu.VMEM((resp_len, 2, HEAD_DIM), jnp.bfloat16),
                    pltpu.SemaphoreType.DMA,
                ],
            ),
            out_shape=jax.ShapeDtypeStruct(queries.shape, jnp.bfloat16),
            input_output_aliases={} if out is None else {8 + 2 * len(blocks): 0},
            compiler_params=params(32),
            cost_estimate=pl.CostEstimate(
                flops=scores * HEAD_DIM * 4,
                bytes_accessed=moved * 8 // slots,
                transcendentals=scores,
            ),
        )(
            place,
            groups,
            resp_lengths,
            prompt_lengths,
            queries,
            resp_kv,
            *own,
            *blocks,
            *blocks,
            *([] if out is None else [out]),
        )
    return out


def solution(mesh):
    return jax.shard_map(
        on_device,
        mesh=mesh,
        in_specs=(
            P(("groups", "dp"), None),
            P(("groups", "dp"), None, None),
            P(("groups", "dp"), None, None),
            P(("groups", "dp")),
            P(("groups", "dp")),
            P("groups"),
        ),
        out_specs=P(("groups", "dp"), None),
        check_vma=False,
    )
```
